256 devices in a mesh: feat: 16 (over y_lo, x, core), batch: 16 (over y_hi, z).
Axes of the slice: x: 4, y: 4 (y_hi: 2, y_lo: 2; y = y_hi * 2 + y_lo), z: 8, core: 2. Of those that a mesh axis runs over, the one named last changes fastest.
Arguments:
- features: bfloat16 [131072, 4096], P('batch', 'feat'), may hold values from -6 to 6
- src_tile: int32 [256, 2], P('batch'), may hold values from 0 to 7
- rel_type: int32 [256, 2], P('batch'), may hold values from 0 to 3
- timestamps: int32 [32768], P(('batch', 'feat')), may hold values from 0 to 127
- edge_tiles: bfloat16 [4, 128, 1024], replicated, may hold values from -0.1875 to 0.1875
- rel_weight: bfloat16 [4, 4096, 512], P(None, 'feat'), may hold values from -0.09375 to 0.09375
- attn_gain: float32 [512], replicated, may hold values from 0.1 to 1.9
- w_qkv: bfloat16 [512, 1536], replicated, as said below
- w_out: bfloat16 [512, 512], replicated, may hold values from -0.25 to 0.25
- cotangent: bfloat16 [32768, 512], P(('batch', 'feat')), may hold values from -96 to 96
Outputs:
- layer_out: bfloat16 [32768, 512], P(('batch', 'feat'))
- grad_qkv: bfloat16 [512, 1536], replicated
- grad_out: bfloat16 [512, 512], replicated
- grad_gain: bfloat16 [512], replicated
- grad_rel: bfloat16 [4, 4096, 512], P(None, 'feat')
The draws below stay inside these ranges and needn't reach their ends.
Inputs may be any that keep to these rules, and one draw needn't show every extreme that they name: `src_tile`: index of a source tile within the batch group. `w_qkv`: query, key and value columns in that order along the second dimension.
All inputs are finite; a program needn't handle non-finite values.
Results may differ from the reference program's by a relative error of at most 0.014.
Values may be sent and summed in bfloat16 or wider, within the bound.
No kernel may reach another device: no remote copies, remote signals or barrier semaphores. Data moves between devices by JAX's collectives and lax.ppermute only.
A program may use at most 128 MiB of HBM per device.

```python
import math
import jax
import jax.numpy as jnp
from jax import lax

F = 4096
D = 512
HEADS = 8
HEAD_DIM = 64
NREL = 4
SLOTS = 2
TBLK = 128
SBLK = 1024
SRC_BLOCKS = 8
ROWS_DEV = 128
ROWS = 2048
NBLK = 16
SRC = 8192
ALL_SRC = 131072
TOKENS = 32768
N_FEAT = 16
N_BATCH = 16


def draw_w_qkv(key, part):
    first = jax.random.fold_in(key, 0)
    whole = jax.random.normal(first, (D, 3 * D), jnp.float32) * D ** (-0.5)
    return whole.astype(jnp.bfloat16)


def draw_cotangent(key, part):
    first, second = jax.random.split(jax.random.fold_in(key, 71), 2)
    base = jnp.clip(jax.random.normal(first, (TOKENS, D), jnp.float32), -4.0, 4.0)
    sequences = TOKENS // ROWS_DEV
    owner = jax.random.permutation(second, D) % sequences
    row_sequence = jnp.arange(TOKENS, dtype=jnp.int32) // ROWS_DEV
    boost = jnp.where(row_sequence[:, None] == owner[None, :].astype(jnp.int32), 24.0, 1.0)
    return (base * boost).astype(jnp.bfloat16)


def with_ends(array, rng, smallest, top_value):
    shape = array.shape
    spot = [jax.random.randint(jax.random.fold_in(rng, axis), (), 0, shape[axis]) for axis in range(len(shape))]
    array = array.at[tuple(spot)].set(smallest)
    longest = shape.index(max(shape))
    spot[longest] = (spot[longest] + 1) % shape[longest]
    return array.at[tuple(spot)].set(top_value)


def steps_of(stream_key, shape, cuts, least, top_value):
    factor_of, own = 1.0, jax.random.fold_in(stream_key, 6)
    for axis_at, blocks in cuts:
        draws = jnp.exp(jax.random.uniform(jax.random.fold_in(own, axis_at), (blocks,), jnp.float32, least / len(cuts), top_value / len(cuts)))
        factor_of = factor_of * jnp.repeat(draws, shape[axis_at] // blocks).reshape([-1 if axis == axis_at else 1 for axis in range(len(shape))])
    return factor_of


def scatter_about(stream_key, dims, spread, most, shards=(), held_as=jnp.bfloat16):
    array = spread * jax.random.normal(stream_key, dims, jnp.float32)
    if shards:
        array = array * steps_of(stream_key, dims, shards, -0.22, 0.18)
    return jnp.clip(array, -most, most).astype(held_as)


def setup_inputs(seed: int = 0) -> dict:
    streams_of = jax.random.split(jax.random.key(seed), 11)
    return {
        "features": scatter_about(streams_of[0], (ALL_SRC, F), 1.0, 6.0, ((0, 16), (1, 16))),
        "src_tile": with_ends(jax.random.randint(streams_of[1], (N_BATCH * NBLK, SLOTS), 0, SRC_BLOCKS), jax.random.fold_in(streams_of[1], 1), 0, SRC_BLOCKS - 1).astype(jnp.int32),
        "rel_type": with_ends(jax.random.randint(streams_of[2], (N_BATCH * NBLK, SLOTS), 0, NREL), jax.random.fold_in(streams_of[2], 1), 0, NREL - 1).astype(jnp.int32),
        "timestamps": with_ends(jax.random.randint(streams_of[3], (TOKENS,), 0, ROWS_DEV), jax.random.fold_in(streams_of[3], 1), 0, ROWS_DEV - 1).astype(jnp.int32),
        "edge_tiles": scatter_about(streams_of[4], (NREL, TBLK, SBLK), SBLK ** -0.5, 0.1875),
        "rel_weight": scatter_about(streams_of[5], (NREL, F, D), F ** -0.5, 0.09375, ((1, 16),)),
        "attn_gain": jnp.clip(1.0 + 0.18 * jax.random.normal(streams_of[6], (D,), jnp.float32), 0.1, 1.9),
        "w_qkv": draw_w_qkv(jax.random.fold_in(streams_of[10], 71), 0),
        "w_out": scatter_about(streams_of[8], (D, D), D ** -0.5, 0.25),
        "cotangent": draw_cotangent(jax.random.fold_in(streams_of[10], 71), 0),
    }


EPS = 1e-06

def aggregate(feats, sources_all, kinds_all, edge_tiles):

    def one_block(pair):
        sources, kinds = pair
        parts = []
        for slot in range(SLOTS):
            piece = lax.dynamic_slice_in_dim(feats, (sources[slot] * SBLK).astype(jnp.int32), SBLK, 0)
            tile = lax.dynamic_index_in_dim(edge_tiles, kinds[slot].astype(jnp.int32), 0, keepdims=False)
            parts.append(jnp.dot(tile, piece, preferred_element_type=jnp.float32))
        member = (kinds[:, None] == jnp.arange(NREL, dtype=jnp.int32)[None, :]).astype(jnp.float32)
        merged = member[0][:, None, None] * parts[0][None]
        for slot in range(1, SLOTS):
            merged = merged + member[slot][:, None, None] * parts[slot][None]
        return merged.astype(jnp.bfloat16)
    blocks = lax.map(one_block, (sources_all, kinds_all))
    return jnp.moveaxis(blocks, 1, 0).reshape(NREL, -1, feats.shape[1])

def layer_forward(tokens, gain, w_qkv, w_out, times):
    token_values = tokens.astype(jnp.float32)
    scale = lax.rsqrt(lax.optimization_barrier(jnp.mean(token_values * token_values, axis=-1, keepdims=True)) + EPS)
    normed = (token_values * scale * gain).astype(jnp.bfloat16)
    projected = jnp.dot(normed, w_qkv, preferred_element_type=jnp.float32).astype(jnp.bfloat16)
    length = tokens.shape[0]
    queries = projected[:, :D].reshape(length, HEADS, HEAD_DIM).astype(jnp.float32)
    keys = projected[:, D:2 * D].reshape(length, HEADS, HEAD_DIM).astype(jnp.float32)
    contents = projected[:, 2 * D:].reshape(length, HEADS, HEAD_DIM).astype(jnp.float32)
    scores = jnp.einsum('qhd,khd->hqk', queries, keys) / math.sqrt(HEAD_DIM)
    allowed = times[None, :] <= times[:, None]
    scores = jnp.where(allowed[None], scores, -1e+30)
    weights = jax.nn.softmax(scores, axis=-1).astype(jnp.bfloat16)
    context = jnp.einsum('hqk,khd->qhd', weights.astype(jnp.float32), contents)
    context = context.astype(jnp.bfloat16).reshape(length, D)
    return (token_values + jnp.dot(context, w_out, preferred_element_type=jnp.float32)).astype(jnp.bfloat16)

def silu_slope(total):
    sigma = jax.nn.sigmoid(total)
    return sigma * (1.0 + total * (1.0 - sigma))

def reference(features, src_tile, rel_type, timestamps, edge_tiles, rel_weight, attn_gain, w_qkv, w_out, cotangent):
    groups = N_BATCH
    feats_all = features.reshape(groups, SRC, F)
    sources_all = src_tile.reshape(groups, NBLK, SLOTS)
    kinds_all = rel_type.reshape(groups, NBLK, SLOTS)
    times_all = timestamps.reshape(groups, N_FEAT, ROWS_DEV)
    cot_all = cotangent.reshape(groups, N_FEAT, ROWS_DEV, D)

    def group_step(carry, inputs):
        acc_qkv, acc_out, acc_gain, acc_rel = carry
        feats, sources, kinds, times, cots = inputs
        relations = aggregate(feats, sources, kinds, edge_tiles)
        total = jnp.dot(relations[0], rel_weight[0], preferred_element_type=jnp.float32)
        for relation in range(1, NREL):
            total = total + jnp.dot(relations[relation], rel_weight[relation], preferred_element_type=jnp.float32)
        hidden = jax.nn.silu(total).astype(jnp.bfloat16)
        sequences = hidden.reshape(N_FEAT, ROWS_DEV, D)

        def one_sequence(args):
            tokens, seq_times, seq_cot = args
            output, pullback = jax.vjp(lambda a, b, c, d: layer_forward(a, b, c, d, seq_times), tokens, attn_gain, w_qkv, w_out)
            return (output, pullback(seq_cot))
        outputs, grads = lax.map(one_sequence, (sequences, times, cots))
        d_tokens, d_gain, d_qkv, d_out = grads
        acc_qkv = acc_qkv + lax.optimization_barrier(jnp.sum(d_qkv.astype(jnp.float32), axis=0))
        acc_out = acc_out + lax.optimization_barrier(jnp.sum(d_out.astype(jnp.float32), axis=0))
        acc_gain = acc_gain + lax.optimization_barrier(jnp.sum(d_gain.astype(jnp.float32), axis=0))
        d_total = (d_tokens.reshape(ROWS, D).astype(jnp.float32) * silu_slope(total)).astype(jnp.bfloat16)
        rel_terms = jnp.stack([jnp.dot(relations[relation].T, d_total, preferred_element_type=jnp.float32) for relation in range(NREL)])
        acc_rel = acc_rel + rel_terms
        return ((acc_qkv, acc_out, acc_gain, acc_rel), outputs.reshape(ROWS, D))
    start = (jnp.zeros((D, 3 * D), jnp.float32), jnp.zeros((D, D), jnp.float32), jnp.zeros((D,), jnp.float32), jnp.zeros((NREL, F, D), jnp.float32))
    sums, outputs = lax.scan(group_step, start, (feats_all, sources_all, kinds_all, times_all, cot_all))
    layer_out = outputs.reshape(TOKENS, D)
    return (layer_out, sums[0].astype(jnp.bfloat16), sums[1].astype(jnp.bfloat16), sums[2].astype(jnp.bfloat16), sums[3].astype(jnp.bfloat16))
```

```python
import jax
import jax.numpy as jnp
from jax import lax
from jax.experimental import pallas as pl
from jax.experimental.pallas import tpu as pltpu
from jax.sharding import Mesh
from jax.sharding import PartitionSpec as P

F = 4096
D = 512
HEADS = 8
HEAD_DIM = 64
NREL = 4
SLOTS = 2
TBLK = 128
SBLK = 1024
TILES = 8
PAIRS = 8
COLS = 256
PIECES = 16
EPS = 1e-06

BF16 = jnp.bfloat16
F32 = jnp.float32


FEAT8 = ("fy", "fx")
BATCH16 = ("by", "bz")


def dot(a, b, ca, cb):
    return lax.dot_general(a, b, (((ca,), (cb,)), ((), ())), preferred_element_type=F32)


def forward_kernel(core, src, rel, feats, edges, weight, combos, keep, send, proj):
    step = pl.program_id(0)
    halves = []
    for half in range(2):
        piece = feats[half * SBLK : (half + 1) * SBLK, :]
        halves.append(dot(edges[...], piece, 1, 0).astype(BF16))
    for r in range(NREL):
        rows = [h[r * TBLK : (r + 1) * TBLK] for h in halves]
        for half in range(2):
            combos[r, 2 * step + half] = rows[half]
        both = dot(jnp.concatenate(rows, axis=0), weight[r], 1, 0)
        for half in range(2):
            proj[r * TILES + 2 * step + half] = both[half * TBLK : (half + 1) * TBLK]

    @pl.when(step == pl.num_programs(0) - 1)
    def _():
        mine = core[0]
        for j in range(PAIRS):
            for out, which in ((send, 1 - mine), (keep, mine)):
                b = 2 * j + which
                first = proj[rel[b, 0] * TILES + src[b, 0]]
                second = proj[rel[b, 1] * TILES + src[b, 1]]
                out[j] = (first + second).astype(BF16)


def forward(core, src, rel, features, edges, weight):
    steps = TILES // 2
    grid = pltpu.PrefetchScalarGridSpec(
        num_scalar_prefetch=3,
        grid=(steps,),
        in_specs=[
            pl.BlockSpec((2 * SBLK, COLS), lambda i, *_: (i, 0)),
            pl.BlockSpec((NREL * TBLK, SBLK), lambda i, *_: (0, 0)),
            pl.BlockSpec((NREL, COLS, D), lambda i, *_: (0, 0, 0)),
        ],
        out_specs=[
            pl.BlockSpec((NREL, TILES, TBLK, COLS), lambda i, *_: (0, 0, 0, 0)),
            pl.BlockSpec((PAIRS, TBLK, D), lambda i, *_: (0, 0, 0)),
            pl.BlockSpec((PAIRS, TBLK, D), lambda i, *_: (0, 0, 0)),
        ],
        scratch_shapes=[pltpu.VMEM((NREL * TILES, TBLK, D), F32)],
    )
    return pl.pallas_call(
        forward_kernel,
        grid_spec=grid,
        out_shape=[
            jax.ShapeDtypeStruct((NREL, TILES, TBLK, COLS), BF16),
            jax.ShapeDtypeStruct((PAIRS, TBLK, D), BF16),
            jax.ShapeDtypeStruct((PAIRS, TBLK, D), BF16),
        ],
        compiler_params=pltpu.CompilerParams(vmem_limit_bytes=40 * 2**20),
        cost_estimate=pl.CostEstimate(flops=3 * 2**30, bytes_accessed=10 * 2**20, transcendentals=0),
        name="forward",
    )(core, src, rel, features, edges, weight)


def stacked(pair, low):
    zero = jnp.zeros_like(pair)
    return jnp.concatenate([jnp.where(low, pair, zero), jnp.where(low, zero, pair)], axis=0)


def side_by_side(both):
    half = both.shape[0] // 2
    return jnp.concatenate([both[:half], both[half:]], axis=1)


def layer_kernel(core, arrived, times, gain, w_qkv, w_out, cot, out, d_total, keep, send, terms):
    total = arrived[0].astype(F32)
    for j in range(1, PAIRS):
        total = total + arrived[j].astype(F32)
    sigma = 1.0 / (1.0 + jnp.exp(-total))
    tokens = (total * sigma).astype(BF16).astype(F32)
    mean = jnp.mean(tokens * tokens, axis=1, keepdims=True)
    scale = lax.rsqrt(mean + EPS)
    scaled = tokens * scale
    gains = gain[...]
    normed = (scaled * gains).astype(BF16)
    projected = dot(normed, w_qkv[...], 1, 0).astype(BF16)

    row_time = jnp.broadcast_to(times[...], (TBLK, TBLK))
    allowed = row_time <= row_time.T
    allowed = jnp.concatenate([allowed.astype(F32)] * 2, axis=0) > 0.5
    low = lax.broadcasted_iota(jnp.int32, (TBLK, 2 * HEAD_DIM), 1) < HEAD_DIM
    inv = 1.0 / (HEAD_DIM**0.5)

    cots = cot[...]
    d_context = dot(cots, w_out[...], 1, 1).astype(BF16)
    contexts = []
    d_q, d_k, d_v = [], [], []
    for h in range(HEADS // 2):
        at = slice(2 * HEAD_DIM * h, 2 * HEAD_DIM * (h + 1))
        q = projected[:, at]
        k = projected[:, D + at.start : D + at.stop]
        v = projected[:, 2 * D + at.start : 2 * D + at.stop]
        q2, k2, v2 = stacked(q, low), stacked(k, low), stacked(v, low)
        scores = dot(q2, k, 1, 1) * inv
        scores = jnp.where(allowed, scores, -1e30)
        top = jnp.max(scores, axis=1, keepdims=True)
        expo = jnp.exp(scores - top)
        soft = expo / jnp.sum(expo, axis=1, keepdims=True)
        weights = soft.astype(BF16)
        contexts.append(dot(side_by_side(weights), v2, 1, 0).astype(BF16))
        dc2 = stacked(d_context[:, at], low)
        d_weights = dot(dc2, v, 1, 1).astype(BF16).astype(F32)
        d_v.append(dot(weights, dc2, 0, 0).astype(BF16))
        d_soft = soft * (d_weights - jnp.sum(d_weights * soft, axis=1, keepdims=True))
        d_scores = (jnp.where(allowed, d_soft, 0.0) * inv).astype(BF16)
        d_q.append(dot(side_by_side(d_scores), k2, 1, 0).astype(BF16))
        d_k.append(dot(d_scores, q2, 0, 0).astype(BF16))
    context = jnp.concatenate(contexts, axis=1)
    out[...] = (tokens + dot(context, w_out[...], 1, 0)).astype(BF16)

    d_projected = jnp.concatenate(d_q + d_k + d_v, axis=1)
    d_normed = dot(d_projected, w_qkv[...], 1, 1).astype(BF16).astype(F32)
    d_gain = jnp.sum(d_normed * scaled, axis=0, keepdims=True)
    inner = d_normed * gains
    along = jnp.sum(inner * tokens, axis=1, keepdims=True)
    d_tokens = cots.astype(F32) + inner * scale - tokens * (scale * scale * scale * along * (1.0 / D))
    slope = sigma * (1.0 + total * (1.0 - sigma))
    d_total[:TBLK] = (d_tokens.astype(BF16).astype(F32) * slope).astype(BF16)
    high = d_gain.astype(BF16).astype(F32)
    row = lax.broadcasted_iota(jnp.int32, (8, D), 0)
    both = jnp.where(row == 0, high, jnp.where(row == 1, d_gain - high, 0.0))
    d_total[TBLK:] = both.astype(BF16)

    d_qkv = dot(normed, d_projected, 0, 0).astype(BF16)
    d_out = dot(context, cots, 0, 0).astype(BF16)
    for p in range(PIECES):
        source, first = (d_qkv, p * 128) if p < 12 else (d_out, (p - 12) * 128)
        terms[:, p] = source[:, first : first + 128].reshape(2 * PAIRS, 32, 128)
    mine = core[0]
    keep[...] = terms[pl.ds(mine * PAIRS, PAIRS)]
    send[...] = terms[pl.ds((1 - mine) * PAIRS, PAIRS)]


def layer(core, arrived, times, gain, w_qkv, w_out, cot):
    smem = pl.BlockSpec(memory_space=pltpu.SMEM)
    vmem = pl.BlockSpec(memory_space=pltpu.VMEM)
    terms = (PAIRS, PIECES, 32, 128)
    return pl.pallas_call(
        layer_kernel,
        in_specs=[smem] + [vmem] * 6,
        out_specs=[vmem] * 4,
        out_shape=[
            jax.ShapeDtypeStruct((TBLK, D), BF16),
            jax.ShapeDtypeStruct((TBLK + 8, D), BF16),
            jax.ShapeDtypeStruct(terms, BF16),
            jax.ShapeDtypeStruct(terms, BF16),
        ],
        scratch_shapes=[pltpu.VMEM((2 * PAIRS, PIECES, 32, 128), BF16)],
        compiler_params=pltpu.CompilerParams(vmem_limit_bytes=40 * 2**20),
        cost_estimate=pl.CostEstimate(flops=2**30, bytes_accessed=8 * 2**20, transcendentals=2**18),
        name="layer",
    )(core, arrived, times, gain, w_qkv, w_out, cot)


def relations_kernel(core, src, rel, own, other, combos, out, summed):
    r = pl.program_id(0)
    mine = core[0]
    summed[...] = jnp.zeros_like(summed)
    for j in range(PAIRS):
        for ref, which in ((own, mine), (other, 1 - mine)):
            b = 2 * j + which
            for slot in range(SLOTS):

                @pl.when(rel[b, slot] == r)
                def _():
                    at = src[b, slot]
                    summed[at] = summed[at] + ref[j, :TBLK].astype(F32)

    rows = summed[...].astype(BF16).reshape(TILES * TBLK, D)
    out[0] = dot(combos[0], rows, 1, 0).astype(BF16)


def relations_grad(core, src, rel, own, other, combos):
    grid = pltpu.PrefetchScalarGridSpec(
        num_scalar_prefetch=3,
        grid=(NREL,),
        in_specs=[
            pl.BlockSpec((PAIRS, TBLK + 8, D), lambda r, *_: (0, 0, 0)),
            pl.BlockSpec((PAIRS, TBLK + 8, D), lambda r, *_: (0, 0, 0)),
            pl.BlockSpec((1, COLS, TILES * TBLK), lambda r, *_: (r, 0, 0)),
        ],
        out_specs=pl.BlockSpec((1, COLS, D), lambda r, *_: (r, 0, 0)),
        scratch_shapes=[pltpu.VMEM((TILES, TBLK, D), F32)],
    )
    return pl.pallas_call(
        relations_kernel,
        grid_spec=grid,
        out_shape=jax.ShapeDtypeStruct((NREL, COLS, D), BF16),
        compiler_params=pltpu.CompilerParams(vmem_limit_bytes=40 * 2**20),
        cost_estimate=pl.CostEstimate(flops=2**30, bytes_accessed=6 * 2**20, transcendentals=0),
        name="relations",
    )(core, src, rel, own, other, combos)


def assemble_kernel(core, own, other, grad_qkv, grad_out):
    mine = core[0]
    for ref, which in ((own, mine), (other, 1 - mine)):
        rows = pl.ds(pl.multiple_of(which * PAIRS * 32, PAIRS * 32), PAIRS * 32)
        for p in range(PIECES):
            target, first = (grad_qkv, p * 128) if p < 12 else (grad_out, (p - 12) * 128)
            target[rows, first : first + 128] = ref[:, p].reshape(PAIRS * 32, 128)


def assemble(core, own, other):
    smem = pl.BlockSpec(memory_space=pltpu.SMEM)
    vmem = pl.BlockSpec(memory_space=pltpu.VMEM)
    return pl.pallas_call(
        assemble_kernel,
        in_specs=[smem, vmem, vmem],
        out_specs=[vmem, vmem],
        out_shape=[jax.ShapeDtypeStruct((D, 3 * D), BF16), jax.ShapeDtypeStruct((D, D), BF16)],
        compiler_params=pltpu.CompilerParams(vmem_limit_bytes=16 * 2**20),
        cost_estimate=pl.CostEstimate(flops=0, bytes_accessed=4 * 2**20, transcendentals=0),
        name="assemble",
    )(core, own, other)


def swap(x, axis):
    return lax.ppermute(x, axis, [(0, 1), (1, 0)])


def exchange(pieces, axes):
    return lax.all_to_all(pieces, axes, split_axis=0, concat_axis=0, tiled=True)


def gather(x, axes):
    devices = lax.axis_size(axes)
    return exchange(jnp.broadcast_to(x[None], (devices, *x.shape)), axes)


def summed(x):
    return x.astype(F32).sum(axis=0)


def shards(features, src, rel, timestamps, edge_tiles, rel_weight, attn_gain, w_qkv, w_out, cotangent):
    core = lax.axis_index("fc").astype(jnp.int32).reshape(1)
    combos, keep, send = forward(
        core, src, rel, features, edge_tiles.reshape(NREL * TBLK, SBLK), rel_weight
    )
    partial = (keep.astype(F32) + swap(send, "fc").astype(F32)).astype(BF16)
    arrived = exchange(partial, FEAT8)
    turned = jnp.swapaxes(combos.reshape(NREL, TILES * TBLK, COLS), 1, 2)

    layer_out, d_total, keep, send = layer(
        core, arrived, timestamps.reshape(1, TBLK), attn_gain.reshape(1, D), w_qkv, w_out, cotangent
    )

    own = gather(d_total, FEAT8)
    other = swap(own, "fc")
    rel_terms = relations_grad(core, src, rel, own, other, turned)
    pieces = exchange(rel_terms.reshape(8, TBLK, D), "bz")
    piece = summed(pieces).astype(BF16)
    piece = (piece.astype(F32) + swap(piece, "by").astype(F32)).astype(BF16)
    grad_rel = gather(piece, "bz").reshape(NREL, COLS, D)

    terms = (keep.astype(F32) + swap(send, "fc").astype(F32)).astype(BF16)
    terms = summed(exchange(terms, FEAT8)).astype(BF16)
    gains = summed(own[:, TBLK:]) + summed(other[:, TBLK:])
    gain = gains[0] + gains[1]
    high = gain.astype(BF16)
    rest = (gain - high.astype(F32)).astype(BF16)
    gain_rows = jnp.concatenate([high.reshape(4, 128), rest.reshape(4, 128)], axis=0)
    gain_rows = jnp.broadcast_to(gain_rows[None], (PIECES, 8, 128))
    over_batch = summed(exchange(jnp.concatenate([terms, gain_rows], axis=1), BATCH16))
    grad_gain = (over_batch[32:36] + over_batch[36:40]).reshape(D).astype(BF16)
    rows = gather(over_batch[:32].astype(BF16), BATCH16)
    own_rows = gather(rows, FEAT8)
    grad_qkv, grad_out = assemble(core, own_rows, swap(own_rows, "fc"))
    return (layer_out, grad_qkv, grad_out, grad_gain, grad_rel)


def solution(mesh):
    split = Mesh(mesh.devices.reshape(2, 4, 2, 2, 8), ("fy", "fx", "fc", "by", "bz"))
    feat = ("fy", "fx", "fc")
    batch = ("by", "bz")
    in_specs = (
        P(batch, feat),
        P(batch, None),
        P(batch, None),
        P(batch + feat),
        P(),
        P(None, feat, None),
        P(),
        P(),
        P(),
        P(batch + feat, None),
    )
    out_specs = (P(batch + feat, None), P(), P(), P(), P(None, feat, None))
    return jax.shard_map(shards, mesh=split, in_specs=in_specs, out_specs=out_specs, check_vma=False)
```

```python
import jax
import jax.numpy as jnp
from jax import lax
from jax.experimental import pallas as pl
from jax.experimental.pallas import tpu as pltpu
from jax.sharding import Mesh
from jax.sharding import PartitionSpec as P

D = 512
HEADS = 8
HEAD_DIM = 64
NREL = 4
SLOTS = 2
TBLK = 128
SBLK = 1024
TILES = 8
PAIRS = 8
COLS = 256
HALF = 64
EPS = 1e-06

BF16 = jnp.bfloat16
F32 = jnp.float32


FEAT8 = ("fy", "fx")
SMEM = pl.BlockSpec(memory_space=pltpu.SMEM)
VMEM = pl.BlockSpec(memory_space=pltpu.VMEM)
HBM = pl.BlockSpec(memory_space=pltpu.MemorySpace.HBM)

SRC, REL, PLACE = 0, SLOTS, 2 * SLOTS
CORE, Y, X, BY = 0, 1, 2, 3


def dot(a, b, ca, cb):
    return lax.dot_general(a, b, (((ca,), (cb,)), ((), ())), preferred_element_type=F32)


def forward_kernel(table, feats, edges, weight, combos, keep, send, tiles, edge, weights, proj, sems):
    copies = [pltpu.make_async_copy(edges, edge, sems.at[TILES])]
    copies[0].start()

    def tile_copy(t):
        return pltpu.make_async_copy(feats.at[pl.ds(t * SBLK, SBLK)], tiles.at[t], sems.at[t])

    for t in range(TILES):
        tile_copy(t).start()
        if t == 1:
            copies.append(pltpu.make_async_copy(weight, weights, sems.at[TILES + 1]))
            copies[1].start()
    copies[0].wait()

    def one_tile(t, _):
        tile_copy(t).wait()
        products = dot(edge[...], tiles[t], 1, 0).astype(BF16)
        for r in range(NREL):
            combos[r, t] = products[r * TBLK : (r + 1) * TBLK]
        return 0

    lax.fori_loop(0, TILES, one_tile, 0)
    copies[1].wait()

    def one_relation(r, _):
        rows = combos[r].reshape(TILES * TBLK, COLS)
        proj[pl.ds(r * TILES, TILES)] = dot(rows, weights[r], 1, 0).reshape(TILES, TBLK, D)
        return 0

    lax.fori_loop(0, NREL, one_relation, 0)
    mine = table[PLACE, CORE]

    def one_block(j, _):
        for out, which in ((send, 1 - mine), (keep, mine)):
            b = 2 * j + which
            first = proj[table[REL, b] * TILES + table[SRC, b]]
            second = proj[table[REL + 1, b] * TILES + table[SRC + 1, b]]
            out[j] = (first + second).astype(BF16)
        return 0

    lax.fori_loop(0, PAIRS, one_block, 0)


def forward(table, features, edges, weight):
    return pl.pallas_call(
        forward_kernel,
        in_specs=[SMEM, HBM, HBM, HBM],
        out_specs=[VMEM] * 3,
        out_shape=[
            jax.ShapeDtypeStruct((NREL, TILES, TBLK, COLS), BF16),
            jax.ShapeDtypeStruct((PAIRS, TBLK, D), BF16),
            jax.ShapeDtypeStruct((PAIRS, TBLK, D), BF16),
        ],
        scratch_shapes=[
            pltpu.VMEM((TILES, SBLK, COLS), BF16),
            pltpu.VMEM((NREL * TBLK, SBLK), BF16),
            pltpu.VMEM((NREL, COLS, D), BF16),
            pltpu.VMEM((NREL * TILES, TBLK, D), F32),
            pltpu.SemaphoreType.DMA((TILES + 2,)),
        ],
        compiler_params=pltpu.CompilerParams(vmem_limit_bytes=51 * 2**20),
        cost_estimate=pl.CostEstimate(flops=3 * 2**30, bytes_accessed=10 * 2**20, transcendentals=0),
        name="forward",
    )(table, features, edges, weight)


def stacked(pair, low):
    zero = jnp.zeros_like(pair)
    return jnp.concatenate([jnp.where(low, pair, zero), jnp.where(low, zero, pair)], axis=0)


def side_by_side(both):
    half = both.shape[0] // 2
    return jnp.concatenate([both[:half], both[half:]], axis=1)


def layer_kernel(table, arrived, times, gain, w_qkv, w_out, cot, out, d_total, keep, send, terms):
    total = arrived[0].astype(F32)
    for j in range(1, PAIRS):
        total = total + arrived[j].astype(F32)
    sigma = 1.0 / (1.0 + jnp.exp(-total))
    tokens = (total * sigma).astype(BF16).astype(F32)
    mean = jnp.mean(tokens * tokens, axis=1, keepdims=True)
    scale = lax.rsqrt(mean + EPS)
    scaled = tokens * scale
    gains = gain[...]
    normed = (scaled * gains).astype(BF16)
    projected = dot(normed, w_qkv[...], 1, 0).astype(BF16)

    row_time = jnp.broadcast_to(times[...], (TBLK, TBLK))
    allowed = row_time <= row_time.T
    allowed = jnp.concatenate([allowed.astype(F32)] * 2, axis=0) > 0.5
    low = lax.broadcasted_iota(jnp.int32, (TBLK, 2 * HEAD_DIM), 1) < HEAD_DIM
    inv = 1.0 / (HEAD_DIM**0.5)

    cots = cot[...]
    d_context = dot(cots, w_out[...], 1, 1).astype(BF16)
    contexts = []
    d_q, d_k, d_v = [], [], []
    for h in range(HEADS // 2):
        at = slice(2 * HEAD_DIM * h, 2 * HEAD_DIM * (h + 1))
        q = projected[:, at]
        k = projected[:, D + at.start : D + at.stop]
        v = projected[:, 2 * D + at.start : 2 * D + at.stop]
        q2, k2, v2 = stacked(q, low), stacked(k, low), stacked(v, low)
        scores = dot(q2, k, 1, 1) * inv
        scores = jnp.where(allowed, scores, -1e30)
        top = jnp.max(scores, axis=1, keepdims=True)
        expo = jnp.exp(scores - top)
        soft = expo / jnp.sum(expo, axis=1, keepdims=True)
        weights = soft.astype(BF16)
        contexts.append(dot(side_by_side(weights), v2, 1, 0).astype(BF16))
        dc2 = stacked(d_context[:, at], low)
        d_weights = dot(dc2, v, 1, 1).astype(BF16).astype(F32)
        d_v.append(dot(weights, dc2, 0, 0).astype(BF16))
        d_soft = soft * (d_weights - jnp.sum(d_weights * soft, axis=1, keepdims=True))
        d_scores = (jnp.where(allowed, d_soft, 0.0) * inv).astype(BF16)
        d_q.append(dot(side_by_side(d_scores), k2, 1, 0).astype(BF16))
        d_k.append(dot(d_scores, q2, 0, 0).astype(BF16))
    context = jnp.concatenate(contexts, axis=1)
    out[...] = (tokens + dot(context, w_out[...], 1, 0)).astype(BF16)

    d_projected = jnp.concatenate(d_q + d_k + d_v, axis=1)
    d_normed = dot(d_projected, w_qkv[...], 1, 1).astype(BF16).astype(F32)
    d_gain = jnp.sum(d_normed * scaled, axis=0, keepdims=True)
    inner = d_normed * gains
    along = jnp.sum(inner * tokens, axis=1, keepdims=True)
    d_tokens = cots.astype(F32) + inner * scale - tokens * (scale * scale * scale * along * (1.0 / D))
    slope = sigma * (1.0 + total * (1.0 - sigma))
    d_total[:TBLK] = (d_tokens.astype(BF16).astype(F32) * slope).astype(BF16)
    high = d_gain.astype(BF16).astype(F32)
    row = lax.broadcasted_iota(jnp.int32, (8, D), 0)
    both = jnp.where(row == 0, high, jnp.where(row == 1, d_gain - high, 0.0))
    d_total[TBLK:] = both.astype(BF16)

    d_qkv = dot(normed, d_projected, 0, 0).astype(BF16)
    d_out = dot(context, cots, 0, 0).astype(BF16)
    for part in range(4):
        source = d_qkv[:, part * D : (part + 1) * D] if part < 3 else d_out
        source = source.reshape(2 * PAIRS, 2, 16, D)
        for half in range(2):
            terms[:, 2 * part + half] = source[:, half]
    mine = table[PLACE, CORE]
    keep[...] = terms[pl.ds(mine * PAIRS, PAIRS)]
    send[...] = terms[pl.ds((1 - mine) * PAIRS, PAIRS)]


def layer(table, arrived, times, gain, w_qkv, w_out, cot):
    terms = (PAIRS, 8, 16, D)
    return pl.pallas_call(
        layer_kernel,
        in_specs=[SMEM] + [VMEM] * 6,
        out_specs=[VMEM] * 4,
        out_shape=[
            jax.ShapeDtypeStruct((TBLK, D), BF16),
            jax.ShapeDtypeStruct((TBLK + 8, D), BF16),
            jax.ShapeDtypeStruct(terms, BF16),
            jax.ShapeDtypeStruct(terms, BF16),
        ],
        scratch_shapes=[pltpu.VMEM((2 * PAIRS, 8, 16, D), BF16)],
        compiler_params=pltpu.CompilerParams(vmem_limit_bytes=28 * 2**20),
        cost_estimate=pl.CostEstimate(flops=2**30, bytes_accessed=8 * 2**20, transcendentals=2**18),
        name="layer",
    )(table, arrived, times, gain, w_qkv, w_out, cot)


def relations_kernel(table, own, other, combos, keep, send, gains, summed, rows):
    mine = table[PLACE, CORE]
    half = pl.multiple_of(table[PLACE, BY] * HALF, HALF)
    rest = pl.multiple_of(HALF - half, HALF)

    total = jnp.zeros((8, D), F32)
    first = jnp.zeros((8, D), F32)
    for j in range(PAIRS):
        first = first + own[j, TBLK:].astype(F32)
        total = total + other[j, TBLK:].astype(F32)
    gains[...] = first + total

    def one_relation(r, _):
        summed[...] = jnp.zeros_like(summed)

        def one_pair(j, _):
            for ref, which in ((own, mine), (other, 1 - mine)):
                b = 2 * j + which
                for slot in range(SLOTS):

                    @pl.when(table[REL + slot, b] == r)
                    def _():
                        at = table[SRC + slot, b]
                        summed[at] = summed[at] + ref[j, :TBLK].astype(F32)

            return 0

        lax.fori_loop(0, PAIRS, one_pair, 0)
        sums = summed[...].astype(BF16).reshape(TILES * TBLK, D)
        rows[...] = dot(combos[r], sums, 1, 0).astype(BF16).reshape(2, TBLK, D)
        keep[pl.ds(2 * r, 2)] = rows[:, pl.ds(half, HALF)]
        send[pl.ds(2 * r, 2)] = rows[:, pl.ds(rest, HALF)]
        return 0

    lax.fori_loop(0, NREL, one_relation, 0)


def relations_grad(table, own, other, combos):
    return pl.pallas_call(
        relations_kernel,
        in_specs=[SMEM] + [VMEM] * 3,
        out_specs=[VMEM] * 3,
        out_shape=[
            jax.ShapeDtypeStruct((8, HALF, D), BF16),
            jax.ShapeDtypeStruct((8, HALF, D), BF16),
            jax.ShapeDtypeStruct((8, D), F32),
        ],
        scratch_shapes=[pltpu.VMEM((TILES, TBLK, D), F32), pltpu.VMEM((2, TBLK, D), BF16)],
        compiler_params=pltpu.CompilerParams(vmem_limit_bytes=24 * 2**20),
        cost_estimate=pl.CostEstimate(flops=2**30, bytes_accessed=6 * 2**20, transcendentals=0),
        name="relations",
    )(table, own, other, combos)


def assemble_kernel(table, *refs):
    own, other, (grad_qkv, grad_out) = refs[:PAIRS], refs[PAIRS : 2 * PAIRS], refs[2 * PAIRS :]
    for k in range(PAIRS):
        dy, dx = shifts(k)
        y, x = lax.rem(table[PLACE, Y] + 2 - dy, 2), lax.rem(table[PLACE, X] + 4 - dx, 4)
        for ref, which in ((own[k], table[PLACE, CORE]), (other[k], 1 - table[PLACE, CORE])):
            first = (which * PAIRS + y * 4 + x) * 32
            for piece in range(8):
                rows = pl.ds(pl.multiple_of(first + (piece % 2) * 16, 16), 16)
                part = piece // 2
                target, at = (grad_qkv, part * D) if part < 3 else (grad_out, 0)
                target[rows, at : at + D] = ref[piece]


def assemble(table, own, other):
    return pl.pallas_call(
        assemble_kernel,
        in_specs=[SMEM] + [VMEM] * (2 * PAIRS),
        out_specs=[VMEM, VMEM],
        out_shape=[jax.ShapeDtypeStruct((D, 3 * D), BF16), jax.ShapeDtypeStruct((D, D), BF16)],
        compiler_params=pltpu.CompilerParams(vmem_limit_bytes=16 * 2**20),
        cost_estimate=pl.CostEstimate(flops=0, bytes_accessed=4 * 2**20, transcendentals=0),
        name="assemble",
    )(table, *own, *other)


def swap(x, axis):
    return lax.ppermute(x, axis, [(0, 1), (1, 0)])


def exchange(pieces, axes):
    return lax.all_to_all(pieces, axes, split_axis=0, concat_axis=0, tiled=True)


def gather(x, axes):
    devices = lax.axis_size(axes)
    return exchange(jnp.broadcast_to(x[None], (devices, *x.shape)), axes)


def shifts(k):
    return k // 4, k % 4


def to_place(x, k):
    dy, dx = shifts(k)
    pairs = [(4 * y + q, 4 * ((y + dy) % 2) + (q + dx) % 4) for y in range(2) for q in range(4)]
    return lax.ppermute(x, FEAT8, pairs)


def added(x, y):
    return (x.astype(F32) + y.astype(F32)).astype(BF16)


def summed(x):
    return x.astype(F32).sum(axis=0)


def after(x, first):
    return lax.optimization_barrier((x, first))[0]


def shards(features, src, rel, timestamps, edge_tiles, rel_weight, attn_gain, w_qkv, w_out, cotangent):
    by = lax.axis_index("by")
    lane = lax.broadcasted_iota(jnp.int32, (1, src.shape[0]), 1)
    place = jnp.where(lane == X, lax.axis_index("fx"), by)
    place = jnp.where(lane == Y, lax.axis_index("fy"), place)
    place = jnp.where(lane == CORE, lax.axis_index("fc"), place).astype(jnp.int32)
    table = jnp.concatenate([src.T, rel.T, place], axis=0)
    combos, keep, send = forward(table, features, edge_tiles.reshape(NREL * TBLK, SBLK), rel_weight)
    arrived = exchange(added(keep, swap(send, "fc")), FEAT8)
    turned = jnp.swapaxes(combos.reshape(NREL, TILES * TBLK, COLS), 1, 2)
    arrived, turned = lax.optimization_barrier((arrived, turned))

    layer_out, d_total, keep, send = layer(
        table, arrived, timestamps.reshape(1, TBLK), attn_gain.reshape(1, D), w_qkv, w_out, cotangent
    )

    own = gather(d_total, FEAT8)
    terms = added(keep, swap(send, "fc"))
    own, terms = lax.optimization_barrier((own, terms))
    terms = exchange(terms, FEAT8)
    keep, send, gains = relations_grad(table, own, swap(own, "fc"), turned)
    rel_terms = added(keep, swap(send, "by"))

    terms = summed(after(terms, keep)).astype(BF16)
    gain = gains[0:1] + gains[1:2]
    high = gain.astype(BF16)
    low = (gain - high.astype(F32)).astype(BF16)
    gain_rows = jnp.concatenate([high, low, jnp.zeros((6, D), BF16)], axis=0)
    gain_rows = jnp.broadcast_to(gain_rows[None], (8, 8, D))

    piece = summed(exchange(jnp.concatenate([rel_terms, terms, gain_rows], axis=1), "bz")).astype(BF16)
    partner = swap(piece, "by")
    term = piece[HALF:].astype(F32) + partner[HALF:].astype(F32)
    gain_row = term[16:17] + term[17:18]
    term = jnp.concatenate([term[:16], jnp.broadcast_to(gain_row, (8, D))], axis=0).astype(BF16)
    terms = gather(term, "bz")
    grad_gain = terms[0, 16]
    terms = terms[:, :16]

    piece, partner = piece[:HALF], partner[:HALF]
    piece = jnp.where(by == 0, jnp.concatenate([piece, partner]), jnp.concatenate([partner, piece]))
    piece, terms = lax.optimization_barrier((piece, terms))
    grad_rel = gather(piece, "bz").reshape(NREL, COLS, D)

    own = [terms] + [to_place(terms, k) for k in range(1, PAIRS)]
    other = [swap(part, "fc") for part in own]
    grad_qkv, grad_out = assemble(table, own, other)
    return (layer_out, grad_qkv, grad_out, grad_gain, grad_rel)


def solution(mesh):
    split = Mesh(mesh.devices.reshape(2, 4, 2, 2, 8), ("fy", "fx", "fc", "by", "bz"))
    feat = ("fy", "fx", "fc")
    batch = ("by", "bz")
    in_specs = (
        P(batch, feat),
        P(batch, None),
        P(batch, None),
        P(batch + feat),
        P(),
        P(None, feat, None),
        P(),
        P(),
        P(),
        P(batch + feat, None),
    )
    out_specs = (P(batch + feat, None), P(), P(), P(), P(None, feat, None))
    return jax.shard_map(shards, mesh=split, in_specs=in_specs, out_specs=out_specs, check_vma=False)
```

```python
import jax
import jax.numpy as jnp
from jax import lax
from jax.experimental import pallas as pl
from jax.experimental.pallas import tpu as pltpu
from jax.sharding import Mesh
from jax.sharding import PartitionSpec as P

D = 512
HEADS = 8
HEAD_DIM = 64
NREL = 4
SLOTS = 2
TBLK = 128
SBLK = 1024
TILES = 8
PAIRS = 8
QUADS = 4
COLS = 256
HALF = 64
EPS = 1e-06

BF16 = jnp.bfloat16
F32 = jnp.float32


FEAT8 = ("fy", "fx")
SMEM = pl.BlockSpec(memory_space=pltpu.SMEM)
VMEM = pl.BlockSpec(memory_space=pltpu.VMEM)
HBM = pl.BlockSpec(memory_space=pltpu.MemorySpace.HBM)

SRC, REL, PLACE = 0, SLOTS, 2 * SLOTS
CORE, X, BY = 0, 1, 2


def dot(a, b, ca, cb):
    return lax.dot_general(a, b, (((ca,), (cb,)), ((), ())), preferred_element_type=F32)


def forward_kernel(table, feats, edges, weight, combos, keep, send, tiles, edge, weights, products, proj, sems):
    def tile_copy(t):
        return pltpu.make_async_copy(feats.at[pl.ds(t * SBLK, SBLK)], tiles.at[t], sems.at[t])

    edge_copy = pltpu.make_async_copy(edges, edge, sems.at[TILES])
    weight_copy = pltpu.make_async_copy(weight, weights, sems.at[TILES + 1])
    edge_copy.start()
    tile_copy(0).start()
    edge_copy.wait()
    tile_copy(1).start()
    for t in range(TILES):
        tile_copy(t).wait()
        if t + 2 < TILES:
            tile_copy(t + 2).start()
        elif t + 2 == TILES:
            weight_copy.start()
        both = dot(edge[...], tiles[t], 1, 0).astype(BF16)
        for r in range(NREL):
            products[r, t] = both[r * TBLK : (r + 1) * TBLK]
    out_copy = pltpu.make_async_copy(products, combos, sems.at[TILES + 2])
    out_copy.start()
    weight_copy.wait()
    for r in range(NREL):
        rows = products[r].reshape(TILES * TBLK, COLS)
        proj[r * TILES : (r + 1) * TILES] = dot(rows, weights[r], 1, 0).reshape(TILES, TBLK, D)
    mine = table[PLACE, CORE]
    for j in range(PAIRS):
        for out, which in ((send, 1 - mine), (keep, mine)):
            b = 2 * j + which
            first = proj[table[REL, b] * TILES + table[SRC, b]]
            second = proj[table[REL + 1, b] * TILES + table[SRC + 1, b]]
            out[j] = (first + second).astype(BF16)
    out_copy.wait()


def forward(table, features, edges, weight):
    return pl.pallas_call(
        forward_kernel,
        in_specs=[SMEM, HBM, HBM, HBM],
        out_specs=[HBM, VMEM, VMEM],
        out_shape=[
            jax.ShapeDtypeStruct((NREL, TILES, TBLK, COLS), BF16),
            jax.ShapeDtypeStruct((PAIRS, TBLK, D), BF16),
            jax.ShapeDtypeStruct((PAIRS, TBLK, D), BF16),
        ],
        scratch_shapes=[
            pltpu.VMEM((TILES, SBLK, COLS), BF16),
            pltpu.VMEM((NREL * TBLK, SBLK), BF16),
            pltpu.VMEM((NREL, COLS, D), BF16),
            pltpu.VMEM((NREL, TILES, TBLK, COLS), BF16),
            pltpu.VMEM((NREL * TILES, TBLK, D), F32),
            pltpu.SemaphoreType.DMA((TILES + 3,)),
        ],
        compiler_params=pltpu.CompilerParams(vmem_limit_bytes=51 * 2**20),
        cost_estimate=pl.CostEstimate(flops=3 * 2**30, bytes_accessed=10 * 2**20, transcendentals=0),
        name="forward",
    )(table, features, edges, weight)


def stacked(pair, low):
    zero = jnp.zeros_like(pair)
    return jnp.concatenate([jnp.where(low, pair, zero), jnp.where(low, zero, pair)], axis=0)


def side_by_side(both):
    half = both.shape[0] // 2
    return jnp.concatenate([both[:half], both[half:]], axis=1)


def layer_kernel(arrived, times, gain, w_qkv, w_out, cot, out, d_total, normed_out, d_projected_out, context_out):
    total = arrived[0].astype(F32)
    for j in range(1, PAIRS):
        total = total + arrived[j].astype(F32)
    sigma = 1.0 / (1.0 + jnp.exp(-total))
    tokens = (total * sigma).astype(BF16).astype(F32)
    mean = jnp.mean(tokens * tokens, axis=1, keepdims=True)
    scale = lax.rsqrt(mean + EPS)
    scaled = tokens * scale
    gains = gain[...]
    normed = (scaled * gains).astype(BF16)
    projected = dot(normed, w_qkv[...], 1, 0).astype(BF16)

    row_time = jnp.broadcast_to(times[...], (TBLK, TBLK))
    allowed = row_time <= row_time.T
    allowed = jnp.concatenate([allowed.astype(F32)] * 2, axis=0) > 0.5
    low = lax.broadcasted_iota(jnp.int32, (TBLK, 2 * HEAD_DIM), 1) < HEAD_DIM
    inv = 1.0 / (HEAD_DIM**0.5)

    cots = cot[...]
    d_context = dot(cots, w_out[...], 1, 1).astype(BF16)
    contexts = []
    d_q, d_k, d_v = [], [], []
    for h in range(HEADS // 2):
        at = slice(2 * HEAD_DIM * h, 2 * HEAD_DIM * (h + 1))
        q = projected[:, at]
        k = projected[:, D + at.start : D + at.stop]
        v = projected[:, 2 * D + at.start : 2 * D + at.stop]
        q2, k2, v2 = stacked(q, low), stacked(k, low), stacked(v, low)
        scores = dot(q2, k, 1, 1) * inv
        scores = jnp.where(allowed, scores, -1e30)
        top = jnp.max(scores, axis=1, keepdims=True)
        expo = jnp.exp(scores - top)
        soft = expo / jnp.sum(expo, axis=1, keepdims=True)
        weights = soft.astype(BF16)
        contexts.append(dot(side_by_side(weights), v2, 1, 0).astype(BF16))
        dc2 = stacked(d_context[:, at], low)
        d_weights = dot(dc2, v, 1, 1).astype(BF16).astype(F32)
        d_v.append(dot(weights, dc2, 0, 0).astype(BF16))
        d_soft = soft * (d_weights - jnp.sum(d_weights * soft, axis=1, keepdims=True))
        d_scores = (jnp.where(allowed, d_soft, 0.0) * inv).astype(BF16)
        d_q.append(dot(side_by_side(d_scores), k2, 1, 0).astype(BF16))
        d_k.append(dot(d_scores, q2, 0, 0).astype(BF16))
    context = jnp.concatenate(contexts, axis=1)
    out[...] = (tokens + dot(context, w_out[...], 1, 0)).astype(BF16)

    d_projected = jnp.concatenate(d_q + d_k + d_v, axis=1)
    d_normed = dot(d_projected, w_qkv[...], 1, 1).astype(BF16).astype(F32)
    d_gain = jnp.sum(d_normed * scaled, axis=0, keepdims=True)
    inner = d_normed * gains
    along = jnp.sum(inner * tokens, axis=1, keepdims=True)
    d_tokens = cots.astype(F32) + inner * scale - tokens * (scale * scale * scale * along * (1.0 / D))
    slope = sigma * (1.0 + total * (1.0 - sigma))
    d_total[:TBLK] = (d_tokens.astype(BF16).astype(F32) * slope).astype(BF16)
    high = d_gain.astype(BF16).astype(F32)
    row = lax.broadcasted_iota(jnp.int32, (8, D), 0)
    both = jnp.where(row == 0, high, jnp.where(row == 1, d_gain - high, 0.0))
    d_total[TBLK:] = both.astype(BF16)

    normed_out[...] = normed
    d_projected_out[...] = d_projected
    context_out[...] = context


def layer(arrived, times, gain, w_qkv, w_out, cot):
    return pl.pallas_call(
        layer_kernel,
        in_specs=[VMEM] * 6,
        out_specs=[VMEM] * 5,
        out_shape=[
            jax.ShapeDtypeStruct((TBLK, D), BF16),
            jax.ShapeDtypeStruct((TBLK + 8, D), BF16),
            jax.ShapeDtypeStruct((TBLK, D), BF16),
            jax.ShapeDtypeStruct((TBLK, 3 * D), BF16),
            jax.ShapeDtypeStruct((TBLK, D), BF16),
        ],
        compiler_params=pltpu.CompilerParams(vmem_limit_bytes=16 * 2**20),
        cost_estimate=pl.CostEstimate(flops=2**30, bytes_accessed=8 * 2**20, transcendentals=2**18),
        name="layer",
    )(arrived, times, gain, w_qkv, w_out, cot)


def terms_kernel(table, normed, d_projected, context, cot, keep, send, terms):
    d_qkv = dot(normed[...], d_projected[...], 0, 0).astype(BF16)
    d_out = dot(context[...], cot[...], 0, 0).astype(BF16)
    for part in range(4):
        source = d_qkv[:, part * D : (part + 1) * D] if part < 3 else d_out
        source = source.reshape(2 * QUADS, 2, 32, D)
        for half in range(2):
            terms[:, 2 * part + half] = source[:, half]
    mine = table[PLACE, CORE]
    keep[...] = terms[pl.ds(mine * QUADS, QUADS)]
    send[...] = terms[pl.ds((1 - mine) * QUADS, QUADS)]


def weight_terms(table, normed, d_projected, context, cot):
    terms = (QUADS, 8, 32, D)
    return pl.pallas_call(
        terms_kernel,
        in_specs=[SMEM] + [VMEM] * 4,
        out_specs=[VMEM] * 2,
        out_shape=[jax.ShapeDtypeStruct(terms, BF16), jax.ShapeDtypeStruct(terms, BF16)],
        scratch_shapes=[pltpu.VMEM((2 * QUADS, 8, 32, D), BF16)],
        compiler_params=pltpu.CompilerParams(vmem_limit_bytes=16 * 2**20),
        cost_estimate=pl.CostEstimate(flops=2**28, bytes_accessed=5 * 2**20, transcendentals=0),
        name="terms",
    )(table, normed, d_projected, context, cot)


def relations_kernel(table, own, other, combos, keep, send, gains, summed, rows):
    mine = table[PLACE, CORE]
    half = pl.multiple_of(table[PLACE, BY] * HALF, HALF)
    rest = pl.multiple_of(HALF - half, HALF)

    total = jnp.zeros((8, D), F32)
    first = jnp.zeros((8, D), F32)
    for j in range(PAIRS):
        first = first + own[j, TBLK:].astype(F32)
        total = total + other[j, TBLK:].astype(F32)
    gains[...] = first + total

    def one_relation(r, _):
        summed[...] = jnp.zeros_like(summed)

        for j in range(PAIRS):
            for ref, which in ((own, mine), (other, 1 - mine)):
                b = 2 * j + which
                for slot in range(SLOTS):

                    @pl.when(table[REL + slot, b] == r)
                    def _():
                        at = table[SRC + slot, b]
                        summed[at] = summed[at] + ref[j, :TBLK].astype(F32)

        sums = summed[...].astype(BF16).reshape(TILES * TBLK, D)
        rows[...] = dot(combos[r], sums, 1, 0).astype(BF16).reshape(2, TBLK, D)
        keep[pl.ds(2 * r, 2)] = rows[:, pl.ds(half, HALF)]
        send[pl.ds(2 * r, 2)] = rows[:, pl.ds(rest, HALF)]
        return 0

    lax.fori_loop(0, NREL, one_relation, 0)


def relations_grad(table, own, other, combos):
    return pl.pallas_call(
        relations_kernel,
        in_specs=[SMEM] + [VMEM] * 3,
        out_specs=[VMEM] * 3,
        out_shape=[
            jax.ShapeDtypeStruct((8, HALF, D), BF16),
            jax.ShapeDtypeStruct((8, HALF, D), BF16),
            jax.ShapeDtypeStruct((8, D), F32),
        ],
        scratch_shapes=[pltpu.VMEM((TILES, TBLK, D), F32), pltpu.VMEM((2, TBLK, D), BF16)],
        compiler_params=pltpu.CompilerParams(vmem_limit_bytes=14 * 2**20),
        cost_estimate=pl.CostEstimate(flops=2**30, bytes_accessed=6 * 2**20, transcendentals=0),
        name="relations",
    )(table, own, other, combos)


def assemble_kernel(table, *refs):
    own, other, (grad_qkv, grad_out) = refs[:QUADS], refs[QUADS : 2 * QUADS], refs[2 * QUADS :]
    for k in range(QUADS):
        x = lax.rem(table[PLACE, X] + 4 - k, 4)
        for ref, which in ((own[k], table[PLACE, CORE]), (other[k], 1 - table[PLACE, CORE])):
            first = (which * QUADS + x) * 64
            for piece in range(8):
                rows = pl.ds(pl.multiple_of(first + (piece % 2) * 32, 32), 32)
                part = piece // 2
                target, at = (grad_qkv, part * D) if part < 3 else (grad_out, 0)
                target[rows, at : at + D] = ref[piece]


def assemble(table, own, other):
    return pl.pallas_call(
        assemble_kernel,
        in_specs=[SMEM] + [VMEM] * (2 * QUADS),
        out_specs=[VMEM, VMEM],
        out_shape=[jax.ShapeDtypeStruct((D, 3 * D), BF16), jax.ShapeDtypeStruct((D, D), BF16)],
        compiler_params=pltpu.CompilerParams(vmem_limit_bytes=12 * 2**20),
        cost_estimate=pl.CostEstimate(flops=0, bytes_accessed=4 * 2**20, transcendentals=0),
        name="assemble",
    )(table, *own, *other)


def swap(x, axis):
    return lax.ppermute(x, axis, [(0, 1), (1, 0)])


def exchange(pieces, axes):
    return lax.all_to_all(pieces, axes, split_axis=0, concat_axis=0, tiled=True)


def gather(x, axes):
    devices = lax.axis_size(axes)
    return exchange(jnp.broadcast_to(x[None], (devices, *x.shape)), axes)


def to_x(x, k):
    return lax.ppermute(x, "fx", [(i, (i + k) % 4) for i in range(4)])


def added(x, y):
    return (x.astype(F32) + y.astype(F32)).astype(BF16)


def summed(x):
    return x.astype(F32).sum(axis=0)


def after(x, first):
    return lax.optimization_barrier((x, first))[0]


def shards(features, src, rel, timestamps, edge_tiles, rel_weight, attn_gain, w_qkv, w_out, cotangent):
    by = lax.axis_index("by")
    lane = lax.broadcasted_iota(jnp.int32, (1, src.shape[0]), 1)
    place = jnp.where(lane == X, lax.axis_index("fx"), by)
    place = jnp.where(lane == CORE, lax.axis_index("fc"), place).astype(jnp.int32)
    table = jnp.concatenate([src.T, rel.T, place], axis=0)
    combos, keep, send = forward(table, features, edge_tiles.reshape(NREL * TBLK, SBLK), rel_weight)
    arrived = exchange(added(keep, swap(send, "fc")), FEAT8)

    layer_out, d_total, normed, d_projected, context = layer(
        arrived, timestamps.reshape(1, TBLK), attn_gain.reshape(1, D), w_qkv, w_out, cotangent
    )

    own = gather(d_total, FEAT8)
    keep, send = weight_terms(table, normed, d_projected, context, cotangent)
    terms = added(keep, swap(send, "fc"))
    turned = jnp.swapaxes(combos.reshape(NREL, TILES * TBLK, COLS), 1, 2)
    own, terms, turned = lax.optimization_barrier((own, terms, turned))
    terms = exchange(terms, "fx")
    keep, send, gains = relations_grad(table, own, swap(own, "fc"), turned)
    rel_terms = added(keep, swap(send, "by"))

    terms = summed(after(terms, keep)).astype(BF16)
    gain = gains[0:1] + gains[1:2]
    high = gain.astype(BF16)
    low = (gain - high.astype(F32)).astype(BF16)
    gain_rows = jnp.concatenate([high, low, jnp.zeros((6, D), BF16)], axis=0)
    gain_rows = jnp.broadcast_to(gain_rows[None], (8, 8, D))

    piece = summed(exchange(jnp.concatenate([rel_terms, terms, gain_rows], axis=1), "bz")).astype(BF16)
    aside = piece[HALF:]
    partner = swap(aside, "by").astype(F32)
    beside = swap(aside[:32], "fy").astype(F32)
    across = lax.ppermute(aside[:32], ("fy", "by"), [(i, 3 - i) for i in range(4)]).astype(F32)
    aside = aside.astype(F32)
    term = (aside[:32] + partner[:32]) + (beside + across)
    gain = aside[32:] + partner[32:]
    gain = jnp.broadcast_to(gain[0:1] + gain[1:2], (8, D))
    rows = gather(jnp.concatenate([piece[:HALF], term.astype(BF16), gain.astype(BF16)], axis=0), "bz")
    grad_gain = rows[0, HALF + 32]
    terms = rows[:, HALF : HALF + 32]

    piece = rows[:, :HALF]
    partner = swap(piece, "by")
    first, second = jnp.where(by == 0, piece, partner), jnp.where(by == 0, partner, piece)
    grad_rel = jnp.stack([first, second], axis=1).reshape(NREL, COLS, D)

    own = [terms] + [to_x(terms, k) for k in range(1, QUADS)]
    other = [swap(part, "fc") for part in own]
    grad_qkv, grad_out = assemble(table, own, other)
    return (layer_out, grad_qkv, grad_out, grad_gain, grad_rel)


def solution(mesh):
    split = Mesh(mesh.devices.reshape(2, 4, 2, 2, 8), ("fy", "fx", "fc", "by", "bz"))
    feat = ("fy", "fx", "fc")
    batch = ("by", "bz")
    in_specs = (
        P(batch, feat),
        P(batch, None),
        P(batch, None),
        P(batch + feat),
        P(),
        P(None, feat, None),
        P(),
        P(),
        P(),
        P(batch + feat, None),
    )
    out_specs = (P(batch + feat, None), P(), P(), P(), P(None, feat, None))
    return jax.shard_map(shards, mesh=split, in_specs=in_specs, out_specs=out_specs, check_vma=False)
```

```python
import functools

import jax
import jax.numpy as jnp
from jax import lax
from jax.experimental import pallas as pl
from jax.experimental.pallas import tpu as pltpu
from jax.sharding import Mesh
from jax.sharding import PartitionSpec as P

D = 512
HEADS = 8
HEAD_DIM = 64
NREL = 4
SLOTS = 2
TBLK = 128
SBLK = 1024
TILES = 8
PAIRS = 8
QUADS = 4
COLS = 256
HALF = 64
EPS = 1e-06

BF16 = jnp.bfloat16
F32 = jnp.float32


FEAT8 = ("fy", "fx")
SMEM = pl.BlockSpec(memory_space=pltpu.SMEM)
VMEM = pl.BlockSpec(memory_space=pltpu.VMEM)
HBM = pl.BlockSpec(memory_space=pltpu.MemorySpace.HBM)

SRC, REL, PLACE = 0, SLOTS, 2 * SLOTS
CORE, X, BY = 0, 1, 2


def dot(a, b, ca, cb):
    return lax.dot_general(a, b, (((ca,), (cb,)), ((), ())), preferred_element_type=F32)


def forward_kernel(table, feats, edges, weight, combos, keep, send, tiles, edge, weights, products, proj, sems):
    def tile_copy(t):
        return pltpu.make_async_copy(feats.at[pl.ds(t * SBLK, SBLK)], tiles.at[t], sems.at[t])

    edge_copy = pltpu.make_async_copy(edges, edge, sems.at[TILES])
    weight_copy = pltpu.make_async_copy(weight, weights, sems.at[TILES + 1])
    edge_copy.start()
    tile_copy(0).start()
    edge_copy.wait()
    tile_copy(1).start()
    for t in range(TILES):
        tile_copy(t).wait()
        if t + 2 < TILES:
            tile_copy(t + 2).start()
        elif t + 2 == TILES:
            weight_copy.start()
        both = dot(edge[...], tiles[t], 1, 0).astype(BF16)
        for r in range(NREL):
            products[r, t] = both[r * TBLK : (r + 1) * TBLK]
    out_copy = pltpu.make_async_copy(products, combos, sems.at[TILES + 2])
    out_copy.start()
    weight_copy.wait()
    for r in range(NREL):
        rows = products[r].reshape(TILES * TBLK, COLS)
        proj[r * TILES : (r + 1) * TILES] = dot(rows, weights[r], 1, 0).reshape(TILES, TBLK, D)
    mine = table[PLACE, CORE]
    for j in range(PAIRS):
        for out, which in ((send, 1 - mine), (keep, mine)):
            b = 2 * j + which
            first = proj[table[REL, b] * TILES + table[SRC, b]]
            second = proj[table[REL + 1, b] * TILES + table[SRC + 1, b]]
            out[j] = (first + second).astype(BF16)
    out_copy.wait()


def forward(table, features, edges, weight):
    return pl.pallas_call(
        forward_kernel,
        in_specs=[SMEM, HBM, HBM, HBM],
        out_specs=[HBM, VMEM, VMEM],
        out_shape=[
            jax.ShapeDtypeStruct((NREL, TILES, TBLK, COLS), BF16),
            jax.ShapeDtypeStruct((PAIRS, TBLK, D), BF16),
            jax.ShapeDtypeStruct((PAIRS, TBLK, D), BF16),
        ],
        scratch_shapes=[
            pltpu.VMEM((TILES, SBLK, COLS), BF16),
            pltpu.VMEM((NREL * TBLK, SBLK), BF16),
            pltpu.VMEM((NREL, COLS, D), BF16),
            pltpu.VMEM((NREL, TILES, TBLK, COLS), BF16),
            pltpu.VMEM((NREL * TILES, TBLK, D), F32),
            pltpu.SemaphoreType.DMA((TILES + 3,)),
        ],
        compiler_params=pltpu.CompilerParams(vmem_limit_bytes=51 * 2**20),
        cost_estimate=pl.CostEstimate(flops=3 * 2**30, bytes_accessed=10 * 2**20, transcendentals=0),
        name="forward",
    )(table, features, edges, weight)


def stacked(pair, low):
    zero = jnp.zeros_like(pair)
    return jnp.concatenate([jnp.where(low, pair, zero), jnp.where(low, zero, pair)], axis=0)


def side_by_side(both):
    half = both.shape[0] // 2
    return jnp.concatenate([both[:half], both[half:]], axis=1)


def layer_kernel(arrived, times, gain, w_qkv, w_out, cot, out, d_total, normed_out, d_projected_out, context_out):
    total = arrived[0].astype(F32)
    for j in range(1, PAIRS):
        total = total + arrived[j].astype(F32)
    sigma = 1.0 / (1.0 + jnp.exp(-total))
    tokens = (total * sigma).astype(BF16).astype(F32)
    mean = jnp.mean(tokens * tokens, axis=1, keepdims=True)
    scale = lax.rsqrt(mean + EPS)
    scaled = tokens * scale
    gains = gain[...]
    normed = (scaled * gains).astype(BF16)
    projected = dot(normed, w_qkv[...], 1, 0).astype(BF16)

    row_time = jnp.broadcast_to(times[...], (TBLK, TBLK))
    allowed = row_time <= row_time.T
    allowed = jnp.concatenate([allowed.astype(F32)] * 2, axis=0) > 0.5
    low = lax.broadcasted_iota(jnp.int32, (TBLK, 2 * HEAD_DIM), 1) < HEAD_DIM
    inv = 1.0 / (HEAD_DIM**0.5)

    cots = cot[...]
    d_context = dot(cots, w_out[...], 1, 1).astype(BF16)
    contexts = []
    d_q, d_k, d_v = [], [], []
    for h in range(HEADS // 2):
        at = slice(2 * HEAD_DIM * h, 2 * HEAD_DIM * (h + 1))
        q = projected[:, at]
        k = projected[:, D + at.start : D + at.stop]
        v = projected[:, 2 * D + at.start : 2 * D + at.stop]
        q2, k2, v2 = stacked(q, low), stacked(k, low), stacked(v, low)
        scores = dot(q2, k, 1, 1) * inv
        scores = jnp.where(allowed, scores, -1e30)
        top = jnp.max(scores, axis=1, keepdims=True)
        expo = jnp.exp(scores - top)
        soft = expo / jnp.sum(expo, axis=1, keepdims=True)
        weights = soft.astype(BF16)
        contexts.append(dot(side_by_side(weights), v2, 1, 0).astype(BF16))
        dc2 = stacked(d_context[:, at], low)
        d_weights = dot(dc2, v, 1, 1).astype(BF16).astype(F32)
        d_v.append(dot(weights, dc2, 0, 0).astype(BF16))
        d_soft = soft * (d_weights - jnp.sum(d_weights * soft, axis=1, keepdims=True))
        d_scores = (jnp.where(allowed, d_soft, 0.0) * inv).astype(BF16)
        d_q.append(dot(side_by_side(d_scores), k2, 1, 0).astype(BF16))
        d_k.append(dot(d_scores, q2, 0, 0).astype(BF16))
    context = jnp.concatenate(contexts, axis=1)
    out[...] = (tokens + dot(context, w_out[...], 1, 0)).astype(BF16)

    d_projected = jnp.concatenate(d_q + d_k + d_v, axis=1)
    d_normed = dot(d_projected, w_qkv[...], 1, 1).astype(BF16).astype(F32)
    d_gain = jnp.sum(d_normed * scaled, axis=0, keepdims=True)
    inner = d_normed * gains
    along = jnp.sum(inner * tokens, axis=1, keepdims=True)
    d_tokens = cots.astype(F32) + inner * scale - tokens * (scale * scale * scale * along * (1.0 / D))
    slope = sigma * (1.0 + total * (1.0 - sigma))
    d_total[:TBLK] = (d_tokens.astype(BF16).astype(F32) * slope).astype(BF16)
    high = d_gain.astype(BF16).astype(F32)
    row = lax.broadcasted_iota(jnp.int32, (8, D), 0)
    both = jnp.where(row == 0, high, jnp.where(row == 1, d_gain - high, 0.0))
    d_total[TBLK:] = both.astype(BF16)

    normed_out[...] = normed
    d_projected_out[...] = d_projected
    context_out[...] = context


def layer(arrived, times, gain, w_qkv, w_out, cot):
    return pl.pallas_call(
        layer_kernel,
        in_specs=[VMEM] * 6,
        out_specs=[VMEM] * 5,
        out_shape=[
            jax.ShapeDtypeStruct((TBLK, D), BF16),
            jax.ShapeDtypeStruct((TBLK + 8, D), BF16),
            jax.ShapeDtypeStruct((TBLK, D), BF16),
            jax.ShapeDtypeStruct((TBLK, 3 * D), BF16),
            jax.ShapeDtypeStruct((TBLK, D), BF16),
        ],
        compiler_params=pltpu.CompilerParams(vmem_limit_bytes=16 * 2**20),
        cost_estimate=pl.CostEstimate(flops=2**30, bytes_accessed=8 * 2**20, transcendentals=2**18),
        name="layer",
    )(arrived, times, gain, w_qkv, w_out, cot)


def terms_kernel(table, normed, d_projected, context, cot, keep, send, terms):
    d_qkv = dot(normed[...], d_projected[...], 0, 0).astype(BF16)
    d_out = dot(context[...], cot[...], 0, 0).astype(BF16)
    for part in range(4):
        source = d_qkv[:, part * D : (part + 1) * D] if part < 3 else d_out
        source = source.reshape(2 * QUADS, 2, 32, D)
        for half in range(2):
            terms[:, 2 * part + half] = source[:, half]
    mine = table[PLACE, CORE]
    keep[...] = terms[pl.ds(mine * QUADS, QUADS)]
    send[...] = terms[pl.ds((1 - mine) * QUADS, QUADS)]


def weight_terms(table, normed, d_projected, context, cot):
    terms = (QUADS, 8, 32, D)
    return pl.pallas_call(
        terms_kernel,
        in_specs=[SMEM] + [VMEM] * 4,
        out_specs=[VMEM] * 2,
        out_shape=[jax.ShapeDtypeStruct(terms, BF16), jax.ShapeDtypeStruct(terms, BF16)],
        scratch_shapes=[pltpu.VMEM((2 * QUADS, 8, 32, D), BF16)],
        compiler_params=pltpu.CompilerParams(vmem_limit_bytes=16 * 2**20),
        cost_estimate=pl.CostEstimate(flops=2**28, bytes_accessed=5 * 2**20, transcendentals=0),
        name="terms",
    )(table, normed, d_projected, context, cot)


def relations_kernel(first, table, own, other, combos, keep, send, gains, summed, rows):
    mine = table[PLACE, CORE]
    half = pl.multiple_of(table[PLACE, BY] * HALF, HALF)
    rest = pl.multiple_of(HALF - half, HALF)

    near = jnp.zeros((8, D), F32)
    far = jnp.zeros((8, D), F32)
    for j in range(PAIRS):
        near = near + own[j, TBLK:].astype(F32)
        far = far + other[j, TBLK:].astype(F32)
    gains[...] = near + far

    def one_relation(i, _):
        summed[...] = jnp.zeros_like(summed)
        for j in range(PAIRS):
            for ref, which in ((own, mine), (other, 1 - mine)):
                b = 2 * j + which
                for slot in range(SLOTS):

                    @pl.when(table[REL + slot, b] == first + i)
                    def _():
                        at = table[SRC + slot, b]
                        summed[at] = summed[at] + ref[j, :TBLK].astype(F32)

        sums = summed[...].astype(BF16).reshape(TILES * TBLK, D)
        rows[...] = dot(combos[first + i], sums, 1, 0).astype(BF16).reshape(2, TBLK, D)
        keep[pl.ds(2 * i, 2)] = rows[:, pl.ds(half, HALF)]
        send[pl.ds(2 * i, 2)] = rows[:, pl.ds(rest, HALF)]
        return 0

    lax.fori_loop(0, NREL // 2, one_relation, 0)


def relations_grad(first, table, own, other, combos):
    return pl.pallas_call(
        functools.partial(relations_kernel, first),
        in_specs=[SMEM] + [VMEM] * 3,
        out_specs=[VMEM] * 3,
        out_shape=[
            jax.ShapeDtypeStruct((4, HALF, D), BF16),
            jax.ShapeDtypeStruct((4, HALF, D), BF16),
            jax.ShapeDtypeStruct((8, D), F32),
        ],
        scratch_shapes=[pltpu.VMEM((TILES, TBLK, D), F32), pltpu.VMEM((2, TBLK, D), BF16)],
        compiler_params=pltpu.CompilerParams(vmem_limit_bytes=14 * 2**20),
        cost_estimate=pl.CostEstimate(flops=2**29, bytes_accessed=6 * 2**20, transcendentals=0),
        name="relations",
    )(table, own, other, combos)


def assemble_kernel(table, *refs):
    own, other, (grad_qkv, grad_out) = refs[:QUADS], refs[QUADS : 2 * QUADS], refs[2 * QUADS :]
    for k in range(QUADS):
        x = lax.rem(table[PLACE, X] + 4 - k, 4)
        for ref, which in ((own[k], table[PLACE, CORE]), (other[k], 1 - table[PLACE, CORE])):
            first = (which * QUADS + x) * 64
            for piece in range(8):
                rows = pl.ds(pl.multiple_of(first + (piece % 2) * 32, 32), 32)
                part = piece // 2
                target, at = (grad_qkv, part * D) if part < 3 else (grad_out, 0)
                target[rows, at : at + D] = ref[piece]


def assemble(table, own, other):
    return pl.pallas_call(
        assemble_kernel,
        in_specs=[SMEM] + [VMEM] * (2 * QUADS),
        out_specs=[VMEM, VMEM],
        out_shape=[jax.ShapeDtypeStruct((D, 3 * D), BF16), jax.ShapeDtypeStruct((D, D), BF16)],
        compiler_params=pltpu.CompilerParams(vmem_limit_bytes=12 * 2**20),
        cost_estimate=pl.CostEstimate(flops=0, bytes_accessed=4 * 2**20, transcendentals=0),
        name="assemble",
    )(table, *own, *other)


def swap(x, axis):
    return lax.ppermute(x, axis, [(0, 1), (1, 0)])


def exchange(pieces, axes):
    return lax.all_to_all(pieces, axes, split_axis=0, concat_axis=0, tiled=True)


def gather(x, axes):
    devices = lax.axis_size(axes)
    return exchange(jnp.broadcast_to(x[None], (devices, *x.shape)), axes)


def to_x(x, k):
    return lax.ppermute(x, "fx", [(i, (i + k) % 4) for i in range(4)])


def added(x, y):
    return (x.astype(F32) + y.astype(F32)).astype(BF16)


def summed(x):
    return x.astype(F32).sum(axis=0)


def after(x, first):
    return lax.optimization_barrier((x, first))[0]


def shards(features, src, rel, timestamps, edge_tiles, rel_weight, attn_gain, w_qkv, w_out, cotangent):
    by = lax.axis_index("by")
    lane = lax.broadcasted_iota(jnp.int32, (1, src.shape[0]), 1)
    place = jnp.where(lane == X, lax.axis_index("fx"), by)
    place = jnp.where(lane == CORE, lax.axis_index("fc"), place).astype(jnp.int32)
    table = jnp.concatenate([src.T, rel.T, place], axis=0)
    combos, keep, send = forward(table, features, edge_tiles.reshape(NREL * TBLK, SBLK), rel_weight)
    arrived = exchange(added(keep, swap(send, "fc")), FEAT8)

    layer_out, d_total, normed, d_projected, context = layer(
        arrived, timestamps.reshape(1, TBLK), attn_gain.reshape(1, D), w_qkv, w_out, cotangent
    )

    own = gather(d_total, FEAT8)
    keep, send = weight_terms(table, normed, d_projected, context, cotangent)
    terms = added(keep, swap(send, "fc"))
    turned = jnp.swapaxes(combos.reshape(NREL, TILES * TBLK, COLS), 1, 2)
    own, terms, turned = lax.optimization_barrier((own, terms, turned))
    terms = exchange(terms, "fx")
    other = swap(own, "fc")
    keep, send, gains = relations_grad(0, table, own, other, turned)
    got = swap(send, "by")
    keep2, send2, _ = relations_grad(NREL // 2, table, own, other, turned)
    rel_terms = jnp.concatenate([added(keep, got), added(keep2, swap(send2, "by"))], axis=0)

    terms = summed(after(terms, keep2)).astype(BF16)
    gain = gains[0:1] + gains[1:2]
    high = gain.astype(BF16)
    low = (gain - high.astype(F32)).astype(BF16)
    gain_rows = jnp.concatenate([high, low, jnp.zeros((6, D), BF16)], axis=0)
    gain_rows = jnp.broadcast_to(gain_rows[None], (8, 8, D))

    piece = summed(exchange(jnp.concatenate([rel_terms, terms, gain_rows], axis=1), "bz")).astype(BF16)
    aside = piece[HALF:]
    partner = swap(aside, "by").astype(F32)
    beside = swap(aside[:32], "fy").astype(F32)
    across = lax.ppermute(aside[:32], ("fy", "by"), [(i, 3 - i) for i in range(4)]).astype(F32)
    aside = aside.astype(F32)
    term = (aside[:32] + partner[:32]) + (beside + across)
    gain = aside[32:] + partner[32:]
    gain = jnp.broadcast_to(gain[0:1] + gain[1:2], (8, D))
    rows = gather(jnp.concatenate([piece[:HALF], term.astype(BF16), gain.astype(BF16)], axis=0), "bz")
    grad_gain = rows[0, HALF + 32]
    terms = rows[:, HALF : HALF + 32]

    piece = rows[:, :HALF]
    partner = swap(piece, "by")
    first, second = jnp.where(by == 0, piece, partner), jnp.where(by == 0, partner, piece)
    grad_rel = jnp.stack([first, second], axis=1).reshape(NREL, COLS, D)

    own = [terms] + [to_x(terms, k) for k in range(1, QUADS)]
    other = [swap(part, "fc") for part in own]
    grad_qkv, grad_out = assemble(table, own, other)
    return (layer_out, grad_qkv, grad_out, grad_gain, grad_rel)


def solution(mesh):
    split = Mesh(mesh.devices.reshape(2, 4, 2, 2, 8), ("fy", "fx", "fc", "by", "bz"))
    feat = ("fy", "fx", "fc")
    batch = ("by", "bz")
    in_specs = (
        P(batch, feat),
        P(batch, None),
        P(batch, None),
        P(batch + feat),
        P(),
        P(None, feat, None),
        P(),
        P(),
        P(),
        P(batch + feat, None),
    )
    out_specs = (P(batch + feat, None), P(), P(), P(), P(None, feat, None))
    return jax.shard_map(shards, mesh=split, in_specs=in_specs, out_specs=out_specs, check_vma=False)
```

```python
import functools

import jax
import jax.numpy as jnp
from jax import lax
from jax.experimental import pallas as pl
from jax.experimental.pallas import tpu as pltpu
from jax.sharding import Mesh
from jax.sharding import PartitionSpec as P

D = 512
HEADS = 8
HEAD_DIM = 64
NREL = 4
SLOTS = 2
TBLK = 128
SBLK = 1024
TILES = 8
PAIRS = 8
QUADS = 4
COLS = 256
HALF = 64
EPS = 1e-06

BF16 = jnp.bfloat16
F32 = jnp.float32


FEAT8 = ("fy", "fx")
SMEM = pl.BlockSpec(memory_space=pltpu.SMEM)
VMEM = pl.BlockSpec(memory_space=pltpu.VMEM)
HBM = pl.BlockSpec(memory_space=pltpu.MemorySpace.HBM)

SRC, REL, PLACE = 0, SLOTS, 2 * SLOTS
CORE, X, BY = 0, 1, 2


def dot(a, b, ca, cb):
    return lax.dot_general(a, b, (((ca,), (cb,)), ((), ())), preferred_element_type=F32)


def forward_kernel(table, feats, edges, weight, combos, keep, send, tiles, edge, weights, products, proj, sems):
    def tile_copy(t):
        return pltpu.make_async_copy(feats.at[pl.ds(t * SBLK, SBLK)], tiles.at[t], sems.at[t])

    edge_copy = pltpu.make_async_copy(edges, edge, sems.at[TILES])
    weight_copy = pltpu.make_async_copy(weight, weights, sems.at[TILES + 1])
    edge_copy.start()
    tile_copy(0).start()
    edge_copy.wait()
    tile_copy(1).start()
    for t in range(TILES):
        tile_copy(t).wait()
        if t + 2 < TILES:
            tile_copy(t + 2).start()
        elif t + 2 == TILES:
            weight_copy.start()
        both = dot(edge[...], tiles[t], 1, 0).astype(BF16)
        for r in range(NREL):
            products[r, t] = both[r * TBLK : (r + 1) * TBLK]
    out_copy = pltpu.make_async_copy(products, combos, sems.at[TILES + 2])
    out_copy.start()
    weight_copy.wait()
    for r in range(NREL):
        rows = products[r].reshape(TILES * TBLK, COLS)
        proj[r * TILES : (r + 1) * TILES] = dot(rows, weights[r], 1, 0).reshape(TILES, TBLK, D)
    mine = table[PLACE, CORE]
    for j in range(PAIRS):
        for out, which in ((send, 1 - mine), (keep, mine)):
            b = 2 * j + which
            first = proj[table[REL, b] * TILES + table[SRC, b]]
            second = proj[table[REL + 1, b] * TILES + table[SRC + 1, b]]
            out[j] = (first + second).astype(BF16)
    out_copy.wait()


def forward(table, features, edges, weight):
    return pl.pallas_call(
        forward_kernel,
        in_specs=[SMEM, HBM, HBM, HBM],
        out_specs=[HBM, VMEM, VMEM],
        out_shape=[
            jax.ShapeDtypeStruct((NREL, TILES, TBLK, COLS), BF16),
            jax.ShapeDtypeStruct((PAIRS, TBLK, D), BF16),
            jax.ShapeDtypeStruct((PAIRS, TBLK, D), BF16),
        ],
        scratch_shapes=[
            pltpu.VMEM((TILES, SBLK, COLS), BF16),
            pltpu.VMEM((NREL * TBLK, SBLK), BF16),
            pltpu.VMEM((NREL, COLS, D), BF16),
            pltpu.VMEM((NREL, TILES, TBLK, COLS), BF16),
            pltpu.VMEM((NREL * TILES, TBLK, D), F32),
            pltpu.SemaphoreType.DMA((TILES + 3,)),
        ],
        compiler_params=pltpu.CompilerParams(vmem_limit_bytes=51 * 2**20),
        cost_estimate=pl.CostEstimate(flops=3 * 2**30, bytes_accessed=10 * 2**20, transcendentals=0),
        name="forward",
    )(table, features, edges, weight)


def stacked(pair, low):
    zero = jnp.zeros_like(pair)
    return jnp.concatenate([jnp.where(low, pair, zero), jnp.where(low, zero, pair)], axis=0)


def side_by_side(both):
    half = both.shape[0] // 2
    return jnp.concatenate([both[:half], both[half:]], axis=1)


def layer_kernel(arrived, times, gain, w_qkv, w_out, cot, out, d_total, normed_out, d_projected_out, context_out):
    total = arrived[0].astype(F32)
    for j in range(1, PAIRS):
        total = total + arrived[j].astype(F32)
    sigma = 1.0 / (1.0 + jnp.exp(-total))
    tokens = (total * sigma).astype(BF16).astype(F32)
    mean = jnp.mean(tokens * tokens, axis=1, keepdims=True)
    scale = lax.rsqrt(mean + EPS)
    scaled = tokens * scale
    gains = gain[...]
    normed = (scaled * gains).astype(BF16)
    projected = dot(normed, w_qkv[...], 1, 0).astype(BF16)

    row_time = jnp.broadcast_to(times[...], (TBLK, TBLK))
    allowed = row_time <= row_time.T
    allowed = jnp.concatenate([allowed.astype(F32)] * 2, axis=0) > 0.5
    low = lax.broadcasted_iota(jnp.int32, (TBLK, 2 * HEAD_DIM), 1) < HEAD_DIM
    inv = 1.0 / (HEAD_DIM**0.5)

    cots = cot[...]
    d_context = dot(cots, w_out[...], 1, 1).astype(BF16)
    contexts = []
    d_q, d_k, d_v = [], [], []
    for h in range(HEADS // 2):
        at = slice(2 * HEAD_DIM * h, 2 * HEAD_DIM * (h + 1))
        q = projected[:, at]
        k = projected[:, D + at.start : D + at.stop]
        v = projected[:, 2 * D + at.start : 2 * D + at.stop]
        q2, k2, v2 = stacked(q, low), stacked(k, low), stacked(v, low)
        scores = dot(q2, k, 1, 1) * inv
        scores = jnp.where(allowed, scores, -1e30)
        top = jnp.max(scores, axis=1, keepdims=True)
        expo = jnp.exp(scores - top)
        soft = expo / jnp.sum(expo, axis=1, keepdims=True)
        weights = soft.astype(BF16)
        contexts.append(dot(side_by_side(weights), v2, 1, 0).astype(BF16))
        dc2 = stacked(d_context[:, at], low)
        d_weights = dot(dc2, v, 1, 1).astype(BF16).astype(F32)
        d_v.append(dot(weights, dc2, 0, 0).astype(BF16))
        d_soft = soft * (d_weights - jnp.sum(d_weights * soft, axis=1, keepdims=True))
        d_scores = (jnp.where(allowed, d_soft, 0.0) * inv).astype(BF16)
        d_q.append(dot(side_by_side(d_scores), k2, 1, 0).astype(BF16))
        d_k.append(dot(d_scores, q2, 0, 0).astype(BF16))
    context = jnp.concatenate(contexts, axis=1)
    out[...] = (tokens + dot(context, w_out[...], 1, 0)).astype(BF16)

    d_projected = jnp.concatenate(d_q + d_k + d_v, axis=1)
    d_normed = dot(d_projected, w_qkv[...], 1, 1).astype(BF16).astype(F32)
    d_gain = jnp.sum(d_normed * scaled, axis=0, keepdims=True)
    inner = d_normed * gains
    along = jnp.sum(inner * tokens, axis=1, keepdims=True)
    d_tokens = cots.astype(F32) + inner * scale - tokens * (scale * scale * scale * along * (1.0 / D))
    slope = sigma * (1.0 + total * (1.0 - sigma))
    d_total[:TBLK] = (d_tokens.astype(BF16).astype(F32) * slope).astype(BF16)
    high = d_gain.astype(BF16).astype(F32)
    row = lax.broadcasted_iota(jnp.int32, (8, D), 0)
    both = jnp.where(row == 0, high, jnp.where(row == 1, d_gain - high, 0.0))
    d_total[TBLK:] = both.astype(BF16)

    normed_out[...] = normed
    d_projected_out[...] = d_projected
    context_out[...] = context


def layer(arrived, times, gain, w_qkv, w_out, cot):
    return pl.pallas_call(
        layer_kernel,
        in_specs=[VMEM] * 6,
        out_specs=[VMEM] * 5,
        out_shape=[
            jax.ShapeDtypeStruct((TBLK, D), BF16),
            jax.ShapeDtypeStruct((TBLK + 8, D), BF16),
            jax.ShapeDtypeStruct((TBLK, D), BF16),
            jax.ShapeDtypeStruct((TBLK, 3 * D), BF16),
            jax.ShapeDtypeStruct((TBLK, D), BF16),
        ],
        compiler_params=pltpu.CompilerParams(vmem_limit_bytes=16 * 2**20),
        cost_estimate=pl.CostEstimate(flops=2**30, bytes_accessed=8 * 2**20, transcendentals=2**18),
        name="layer",
    )(arrived, times, gain, w_qkv, w_out, cot)


def terms_kernel(table, normed, d_projected, context, cot, keep, send, terms):
    d_qkv = dot(normed[...], d_projected[...], 0, 0).astype(BF16)
    d_out = dot(context[...], cot[...], 0, 0).astype(BF16)
    for part in range(4):
        source = d_qkv[:, part * D : (part + 1) * D] if part < 3 else d_out
        source = source.reshape(2 * QUADS, 2, 32, D)
        for half in range(2):
            terms[:, 2 * part + half] = source[:, half]
    mine = table[PLACE, CORE]
    keep[...] = terms[pl.ds(mine * QUADS, QUADS)]
    send[...] = terms[pl.ds((1 - mine) * QUADS, QUADS)]


def weight_terms(table, normed, d_projected, context, cot):
    terms = (QUADS, 8, 32, D)
    return pl.pallas_call(
        terms_kernel,
        in_specs=[SMEM] + [VMEM] * 4,
        out_specs=[VMEM] * 2,
        out_shape=[jax.ShapeDtypeStruct(terms, BF16), jax.ShapeDtypeStruct(terms, BF16)],
        scratch_shapes=[pltpu.VMEM((2 * QUADS, 8, 32, D), BF16)],
        compiler_params=pltpu.CompilerParams(vmem_limit_bytes=16 * 2**20),
        cost_estimate=pl.CostEstimate(flops=2**28, bytes_accessed=5 * 2**20, transcendentals=0),
        name="terms",
    )(table, normed, d_projected, context, cot)


def relations_kernel(first, table, own, other, combos, keep, send, gains, summed, rows):
    mine = table[PLACE, CORE]
    half = pl.multiple_of(table[PLACE, BY] * HALF, HALF)
    rest = pl.multiple_of(HALF - half, HALF)

    near = jnp.zeros((8, D), F32)
    far = jnp.zeros((8, D), F32)
    for j in range(PAIRS):
        near = near + own[j, TBLK:].astype(F32)
        far = far + other[j, TBLK:].astype(F32)
    gains[...] = near + far

    def one_relation(i, _):
        summed[...] = jnp.zeros_like(summed)
        for j in range(PAIRS):
            for ref, which in ((own, mine), (other, 1 - mine)):
                b = 2 * j + which
                for slot in range(SLOTS):

                    @pl.when(table[REL + slot, b] == first + i)
                    def _():
                        at = table[SRC + slot, b]
                        summed[at] = summed[at] + ref[j, :TBLK].astype(F32)

        sums = summed[...].astype(BF16).reshape(TILES * TBLK, D)
        rows[...] = dot(combos[first + i], sums, 1, 0).astype(BF16).reshape(2, TBLK, D)
        keep[pl.ds(2 * i, 2)] = rows[:, pl.ds(half, HALF)]
        send[pl.ds(2 * i, 2)] = rows[:, pl.ds(rest, HALF)]
        return 0

    lax.fori_loop(0, NREL // 2, one_relation, 0)


def relations_grad(first, table, own, other, combos):
    return pl.pallas_call(
        functools.partial(relations_kernel, first),
        in_specs=[SMEM] + [VMEM] * 3,
        out_specs=[VMEM] * 3,
        out_shape=[
            jax.ShapeDtypeStruct((4, HALF, D), BF16),
            jax.ShapeDtypeStruct((4, HALF, D), BF16),
            jax.ShapeDtypeStruct((8, D), F32),
        ],
        scratch_shapes=[pltpu.VMEM((TILES, TBLK, D), F32), pltpu.VMEM((2, TBLK, D), BF16)],
        compiler_params=pltpu.CompilerParams(vmem_limit_bytes=14 * 2**20),
        cost_estimate=pl.CostEstimate(flops=2**29, bytes_accessed=6 * 2**20, transcendentals=0),
        name="relations",
    )(table, own, other, combos)


def assemble_kernel(table, *refs):
    own, other, (grad_qkv, grad_out) = refs[:QUADS], refs[QUADS : 2 * QUADS], refs[2 * QUADS :]
    for k in range(QUADS):
        x = lax.rem(table[PLACE, X] + 4 - k, 4)
        for ref, which in ((own[k], table[PLACE, CORE]), (other[k], 1 - table[PLACE, CORE])):
            first = (which * QUADS + x) * 64
            for piece in range(8):
                rows = pl.ds(pl.multiple_of(first + (piece % 2) * 32, 32), 32)
                part = piece // 2
                target, at = (grad_qkv, part * D) if part < 3 else (grad_out, 0)
                target[rows, at : at + D] = ref[piece]


def assemble(table, own, other):
    return pl.pallas_call(
        assemble_kernel,
        in_specs=[SMEM] + [VMEM] * (2 * QUADS),
        out_specs=[VMEM, VMEM],
        out_shape=[jax.ShapeDtypeStruct((D, 3 * D), BF16), jax.ShapeDtypeStruct((D, D), BF16)],
        compiler_params=pltpu.CompilerParams(vmem_limit_bytes=12 * 2**20),
        cost_estimate=pl.CostEstimate(flops=0, bytes_accessed=4 * 2**20, transcendentals=0),
        name="assemble",
    )(table, *own, *other)


def swap(x, axis):
    return lax.ppermute(x, axis, [(0, 1), (1, 0)])


def exchange(pieces, axes):
    return lax.all_to_all(pieces, axes, split_axis=0, concat_axis=0, tiled=True)


def gather(x, axes):
    devices = lax.axis_size(axes)
    return exchange(jnp.broadcast_to(x[None], (devices, *x.shape)), axes)


def to_x(x, k):
    return lax.ppermute(x, "fx", [(i, (i + k) % 4) for i in range(4)])


def added(x, y):
    return (x.astype(F32) + y.astype(F32)).astype(BF16)


def summed(x):
    return x.astype(F32).sum(axis=0)


def two_rows(x):
    high = x.astype(BF16)
    low = (x - high.astype(F32)).astype(BF16)
    return jnp.concatenate([high, low, jnp.zeros((6, D), BF16)], axis=0)


def after(x, first):
    return lax.optimization_barrier((x, first))[0]


def shards(features, src, rel, timestamps, edge_tiles, rel_weight, attn_gain, w_qkv, w_out, cotangent):
    by = lax.axis_index("by")
    lane = lax.broadcasted_iota(jnp.int32, (1, src.shape[0]), 1)
    place = jnp.where(lane == X, lax.axis_index("fx"), by)
    place = jnp.where(lane == CORE, lax.axis_index("fc"), place).astype(jnp.int32)
    table = jnp.concatenate([src.T, rel.T, place], axis=0)
    combos, keep, send = forward(table, features, edge_tiles.reshape(NREL * TBLK, SBLK), rel_weight)
    arrived = exchange(added(keep, swap(send, "fc")), FEAT8)

    layer_out, d_total, normed, d_projected, context = layer(
        arrived, timestamps.reshape(1, TBLK), attn_gain.reshape(1, D), w_qkv, w_out, cotangent
    )

    own = gather(d_total, FEAT8)
    keep, send = weight_terms(table, normed, d_projected, context, cotangent)
    terms = added(keep, swap(send, "fc"))
    turned = jnp.swapaxes(combos.reshape(NREL, TILES * TBLK, COLS), 1, 2)
    own, terms, turned = lax.optimization_barrier((own, terms, turned))
    terms = exchange(terms, "fx")
    other = swap(own, "fc")
    keep, send, gains = relations_grad(0, table, own, other, turned)
    got = swap(send, "by")
    keep2, send2, _ = relations_grad(NREL // 2, table, own, other, turned)
    first_half = added(keep, got)
    got = swap(send2, "by")
    rel_terms = jnp.concatenate([first_half, added(keep2, got)], axis=0)

    terms = summed(after(terms, keep2)).astype(BF16)
    rel_terms, gain_rows = lax.optimization_barrier((rel_terms, two_rows(gains[0:1] + gains[1:2])))

    piece = summed(exchange(jnp.concatenate([rel_terms, terms], axis=1), "bz")).astype(BF16)
    aside = jnp.concatenate([piece[HALF:], gain_rows], axis=0)
    partner = swap(aside, "by").astype(F32)
    beside = swap(aside[:32], "fy").astype(F32)
    across = lax.ppermute(aside[:32], ("fy", "by"), [(i, 3 - i) for i in range(4)]).astype(F32)
    aside = aside.astype(F32)
    term = (aside[:32] + partner[:32]) + (beside + across)
    gain = aside[32:34] + partner[32:34]
    gain_rows = two_rows(gain[0:1] + gain[1:2])
    rows = gather(jnp.concatenate([piece[:HALF], term.astype(BF16), gain_rows], axis=0), "bz")
    gains = summed(rows[:, HALF + 32 : HALF + 34])
    grad_gain = (gains[0] + gains[1]).astype(BF16)
    terms = rows[:, HALF : HALF + 32]

    piece = rows[:, :HALF]
    partner = swap(piece, "by")
    first, second = jnp.where(by == 0, piece, partner), jnp.where(by == 0, partner, piece)
    grad_rel = jnp.stack([first, second], axis=1).reshape(NREL, COLS, D)

    own = [terms] + [to_x(terms, k) for k in range(1, QUADS)]
    other = [swap(part, "fc") for part in own]
    grad_qkv, grad_out = assemble(table, own, other)
    return (layer_out, grad_qkv, grad_out, grad_gain, grad_rel)


def solution(mesh):
    split = Mesh(mesh.devices.reshape(2, 4, 2, 2, 8), ("fy", "fx", "fc", "by", "bz"))
    feat = ("fy", "fx", "fc")
    batch = ("by", "bz")
    in_specs = (
        P(batch, feat),
        P(batch, None),
        P(batch, None),
        P(batch + feat),
        P(),
        P(None, feat, None),
        P(),
        P(),
        P(),
        P(batch + feat, None),
    )
    out_specs = (P(batch + feat, None), P(), P(), P(), P(None, feat, None))
    return jax.shard_map(shards, mesh=split, in_specs=in_specs, out_specs=out_specs, check_vma=False)
```
